512 devices in a mesh: blk: 64 (over y_lo, z, x), row: 8 (over y_hi, core).
Axes of the slice: x: 4, y: 8 (y_hi: 4, y_lo: 2; y = y_hi * 2 + y_lo), z: 8, core: 2. Of those that a mesh axis runs over, the one named last changes fastest.
Arguments:
- points: bfloat16 [65536, 128], P(('blk', 'row')), may hold values from -6 to 6
- w_in: bfloat16 [128, 1024], replicated, may hold values from -0.5 to 0.5
- b_in: float32 [1024], replicated, may hold values from -4 to 4
- w_out: bfloat16 [1024, 128], replicated, may hold values from -0.1875 to 0.1875
- scales: float32 [128], replicated, may hold values from 0.04 to 0.16
- left: bfloat16 [65536, 64], P(('blk', 'row')), may hold values from -2 to 2
- right: bfloat16 [65536, 64], P(('blk', 'row')), may hold values from -2 to 2
Outputs:
- feat_grad: float32 [65536, 128], P(('blk', 'row'))
- grad_w_in: float32 [128, 1024], replicated
- grad_b_in: float32 [1024], replicated
- grad_w_out: float32 [1024, 128], replicated
The draws below stay inside these ranges and needn't reach their ends.
All inputs are finite; a program needn't handle non-finite values.
Results may differ from the reference program's by a relative error of at most 0.012.
The reference program's roundings to bfloat16 on the way (of `hidden`, `scaled`, `pairs_ab`, `weight_b`, `feat_grad_b` and `pre_grad_b`) count: a program that leaves them out, or rounds other values in their place, can miss the bound.
Values may be sent and summed in bfloat16 or wider, within the bound.
A program may use at most 64 MiB of HBM per device.

```python
import math
import jax
import jax.numpy as jnp
from jax import lax

DIN = 128
HID = 1024
FEAT = 128
SOLVE = 64
PB = 1024
NPTS = 65536


def level_of(stream_key, shape, cuts, low, top_value):
    gain = 1.0
    for position, shards_of in cuts:
        draws = jax.random.uniform(jax.random.fold_in(jax.random.fold_in(stream_key, 6), position), (shards_of,), jnp.float32, low / len(cuts), top_value / len(cuts))
        gain = gain * jnp.repeat(jnp.exp(draws), shape[position] // shards_of).reshape((-1,) + (1,) * (len(shape) - 1 - position))
    return gain


def noise(stream_key, dims, width, limit, pieces=(), held_as=jnp.bfloat16):
    drawn = width * jax.random.normal(stream_key, dims, jnp.float32)
    if pieces:
        drawn = drawn * level_of(stream_key, dims, pieces, -0.22, 0.18)
    return jnp.clip(drawn, -limit, limit).astype(held_as)


def setup_inputs(seed: int = 0) -> dict:
    key_of = jax.random.split(jax.random.key(seed), 8)
    points = noise(key_of[0], (NPTS, DIN), 1.0, 6.0, ((0, 512),))
    w_in = noise(key_of[1], (DIN, HID), DIN ** -0.5, 0.5)
    b_in = noise(key_of[2], (HID,), 1.0, 4.0, (), jnp.float32)
    w_out = noise(key_of[3], (HID, FEAT), HID ** -0.5, 0.1875)
    scales = jnp.clip(jnp.exp(jax.random.uniform(key_of[4], (FEAT,), jnp.float32, math.log(0.04), math.log(0.16))), 0.04, 0.16)
    left = noise(key_of[5], (NPTS, SOLVE), 0.25, 2.0, ((0, 512),))
    right = noise(key_of[6], (NPTS, SOLVE), 0.25, 2.0, ((0, 512),))
    return {"points": points, "w_in": w_in, "b_in": b_in, "w_out": w_out, "scales": scales, "left": left, "right": right}


def silu_slope(pre):
    sig = jax.nn.sigmoid(pre)
    return sig * (1.0 + pre * (1.0 - sig))


def reference(points, w_in, b_in, w_out, scales, left, right):
    pre = jnp.dot(points, w_in, preferred_element_type=jnp.float32) + b_in
    hidden = jax.nn.silu(pre).astype(jnp.bfloat16)
    feats = jnp.dot(hidden, w_out, preferred_element_type=jnp.float32)
    scaled = (feats * scales).astype(jnp.bfloat16)
    pairs_ab = jnp.concatenate([left, right], axis=1).astype(jnp.float32)
    pairs_ba = jnp.concatenate([right, left], axis=1).astype(jnp.float32)
    upper = scaled.astype(jnp.float32)
    norms = jnp.sum(upper * upper, axis=1)
    blocks = NPTS // PB
    up_blocks = upper.reshape(blocks, PB, FEAT)
    norm_blocks = norms.reshape(blocks, PB)
    ba_blocks = pairs_ba.reshape(blocks, PB, 2 * SOLVE)

    def one_row_block(index):
        rows_g = lax.dynamic_slice_in_dim(upper, index * PB, PB, 0)
        rows_n = lax.dynamic_slice_in_dim(norms, index * PB, PB, 0)
        rows_ab = lax.dynamic_slice_in_dim(pairs_ab, index * PB, PB, 0)

        def over_columns(total, cols):
            cols_g, cols_n, cols_ba = cols
            cross = jnp.dot(rows_g, cols_g.T, precision=lax.Precision.HIGHEST)
            dist = rows_n[:, None] + cols_n[None, :] - 2.0 * cross
            kern = jnp.exp(-0.5 * dist)
            coup = jnp.dot(rows_ab, cols_ba.T, precision=lax.Precision.HIGHEST)
            weight = coup * kern
            weight_b = weight.astype(jnp.bfloat16).astype(jnp.float32)
            term = -jnp.sum(weight, axis=1)[:, None] * rows_g + jnp.dot(weight_b, cols_g, precision=lax.Precision.HIGHEST)
            return total + term, None

        start = jnp.zeros((PB, FEAT), jnp.float32)
        total, unused = lax.scan(over_columns, start, (up_blocks, norm_blocks, ba_blocks))
        return total

    scaled_grad = lax.map(one_row_block, jnp.arange(blocks, dtype=jnp.int32)).reshape(NPTS, FEAT)
    feat_grad = scaled_grad * scales
    feat_grad_b = feat_grad.astype(jnp.bfloat16)
    factor = NPTS ** -0.5
    grad_w_out = factor * jnp.dot(hidden.T, feat_grad_b, preferred_element_type=jnp.float32)
    pre_grad = jnp.dot(feat_grad_b, w_out.T, preferred_element_type=jnp.float32) * silu_slope(pre)
    pre_grad_b = pre_grad.astype(jnp.bfloat16)
    grad_w_in = factor * jnp.dot(points.T, pre_grad_b, preferred_element_type=jnp.float32)
    grad_b_in = factor * jnp.sum(pre_grad, axis=0)
    return feat_grad, grad_w_in, grad_b_in, grad_w_out
```

```python
import jax
import jax.numpy as jnp
from jax import lax
from jax.experimental import pallas as pl
from jax.experimental.pallas import tpu as pltpu
from jax.sharding import PartitionSpec as P

NX, NY, NZ, NC = 4, 8, 8, 2
PT = 128
PR = 144
D = 128
HID = 1024
HALF = 512
BF = jnp.bfloat16
F32 = jnp.float32
MESH = pl.DeviceIdType.MESH
NT = (((1,), (1,)), ((), ()))


def split3(v):
    hi = v.astype(BF)
    rest = v - hi.astype(F32)
    mid = rest.astype(BF)
    lo = (rest - mid.astype(F32)).astype(BF)
    return hi, mid, lo


def body(
    points, w_in, b_in, w_out, scales, left, right,
    fg_out, gi_out, gb_out, go_out,
    slope, hid_t, pts_t, rows, cols, rg, rb, ni, acc, sw, t_send, t_in,
    g, x_in, s1, in1, in2, in3, fin,
    send_y, recv_y, send_x, recv_x, send_z, recv_z, send_p, recv_p,
    send_t, recv_t, send_c, recv_c, send_1, recv_1, send_2, recv_2, send_3, recv_3, send_4, recv_4,
):
    blk = lax.axis_index("blk")
    row = lax.axis_index("row")
    y_lo = blk // (NX * NZ)
    z = (blk // NX) % NZ
    x = blk % NX
    c = row % 2
    y = (row // 2) * 2 + y_lo

    def dev(y_, z_, x_, c_):
        return (((y_ % 2) * NZ + z_) * NX + x_, (y_ // 2) * 2 + c_)

    def at_y(k):
        return dev(k, z, x, c)

    def at_z(k):
        return dev(y, k, x, c)

    def at_x(k):
        return dev(y, z, k, c)

    partner = dev(y, z, x, 1 - c)
    nxt = at_z((z + 1) % NZ)
    prv = at_z((z + NZ - 1) % NZ)

    def remote(src, dst, ss, rs, device):
        return pltpu.make_async_remote_copy(
            src_ref=src, dst_ref=dst, send_sem=ss, recv_sem=rs, device_id=device, device_id_type=MESH
        )

    bar = pltpu.get_barrier_semaphore()

    def hello(device):
        pl.semaphore_signal(bar, inc=1, device_id=device, device_id_type=MESH)

    hello(partner)
    for k in range(1, NX):
        hello(at_x((x + k) % NX))
    for k in range(1, NZ):
        hello(at_z((z + k) % NZ))
    for k in range(1, NY):
        hello(at_y((y + k) % NY))

    pts = points[...]
    pre = jnp.dot(pts, w_in[...], preferred_element_type=F32) + b_in[...]
    sig = jax.nn.sigmoid(pre)
    hidden = (pre * sig).astype(BF)
    feats = jnp.dot(hidden, w_out[...], preferred_element_type=F32)
    scaled = (feats * scales[...]).astype(BF)
    sf = scaled.astype(F32)
    sq = sf * sf
    sq_hi = sq.astype(BF)
    sq_lo = (sq - sq_hi.astype(F32)).astype(BF)
    ones = jnp.full((16, D), 0.5, BF)
    norm = lax.dot_general(ones, sq_hi, NT, preferred_element_type=F32) + lax.dot_general(
        ones, sq_lo, NT, preferred_element_type=F32
    )
    hi, mid, lo = split3(norm)
    which = lax.broadcasted_iota(jnp.int32, (16, D), 0)
    zero = jnp.zeros((16, D), F32)
    tail = jnp.where(
        which == 0, hi.astype(F32), jnp.where(which == 1, mid.astype(F32), jnp.where(which == 2, lo.astype(F32), zero))
    ).astype(BF)
    mine = cols.at[c, z, x]
    mine[0:PT, 0:D] = scaled
    mine[0:PT, D : D + 64] = left[...]
    mine[0:PT, D + 64 : 2 * D] = right[...]
    mine[PT:PR, 0:D] = tail
    mine[PT:PR, D : 2 * D] = jnp.zeros((16, D), BF)

    pl.semaphore_wait(bar, 1 + (NX - 1) + (NZ - 1) + (NY - 1))

    def slot_y(k):
        return jnp.where(k == 4, 7, jnp.where(k == 0, 0, jnp.where(k > 4, 2 * (8 - k) - 1, 2 * k)))

    def z_right(zz, xx):
        return remote(cols.at[c, zz, xx], cols.at[c, zz, xx], send_z.at[0, zz, xx], recv_z.at[zz, xx], nxt)

    def z_left(zz, xx):
        return remote(cols.at[c, zz, xx], cols.at[c, zz, xx], send_z.at[1, zz, xx], recv_z.at[zz, xx], prv)

    def to_partner(zz, xx):
        return remote(cols.at[c, zz, xx], cols.at[c, zz, xx], send_p.at[zz, xx], recv_p.at[zz, xx], partner)

    def from_partner(zz, xx):
        return remote(cols.at[1 - c, zz, xx], cols.at[1 - c, zz, xx], send_p.at[zz, xx], recv_p.at[zz, xx], partner)

    def x_copy(k):
        return remote(mine, mine, send_x.at[k], recv_x.at[x], at_x((x + k) % NX))

    def x_from(xx):
        return remote(mine, cols.at[c, z, xx], send_x.at[0], recv_x.at[xx], partner)

    def y_copy(k):
        return remote(mine, rows.at[slot_y((8 - k) % 8)], send_y.at[k], recv_y.at[slot_y((8 - k) % 8)], at_y((y + k) % NY))

    def y_from(s):
        return remote(mine, rows.at[s], send_y.at[0], recv_y.at[s], partner)

    z_right(z, x).start()
    z_left(z, x).start()
    for k in (1, 3, 2):
        x_copy(k).start()
    to_partner(z, x).start()
    for k in (1, 7, 2, 6, 3, 5, 4):
        y_copy(k).start()

    rows[0] = mine[...]
    slope[...] = sig * (1.0 + pre * (1.0 - sig))
    hid_t[...] = hidden.astype(F32).T.astype(BF)
    pts_t[...] = pts.astype(F32).T.astype(BF)

    for k in (1, 3, 2):
        xx = (x + k) % NX
        x_from(xx).wait_recv()
        z_right(z, xx).start()
        z_left(z, xx).start()
        to_partner(z, xx).start()

    acc[...] = jnp.zeros_like(acc)
    sw[...] = jnp.zeros_like(sw)

    def ready_rows(s):
        if s > 0:
            y_from(s).wait_recv()
        gg = rows[s, 0:PT, 0:D]
        ab = rows[s, 0:PT, D : 2 * D].astype(F32)
        at = pl.ds(s * PT, PT)
        rg[at, :] = gg
        rb[at, :] = pltpu.roll(ab, 64, 1).astype(BF)
        gf = gg.astype(F32)
        ni[at, :] = jnp.broadcast_to(0.5 * jnp.sum(gf * gf, axis=1, keepdims=True), (PT, D))

    for s in range(4):
        ready_rows(s)

    def unit(t):
        edge = jnp.logical_or(t == 0, t == 7)
        dist = (t + 1) // 2
        return edge, dist

    def block_of(t, way):
        edge, dist = unit(t)
        zz = jnp.where(way == 0, (z + NZ - dist) % NZ, (z + dist) % NZ)
        h = jnp.where(edge, way, (t + 1) % 2)
        return zz, h

    def arrivals(t):
        _, dist = unit(t)
        for way in (0, 1):
            zz, h = block_of(t, way)
            on = jnp.logical_or(dist + 1 < 4, jnp.logical_and(dist == 3, h == way))
            for i in (0, 1):
                xx = 2 * h + i
                hop = z_right(zz, xx) if way == 0 else z_left(zz, xx)
                hop.wait_recv()

                @pl.when(on)
                def _():
                    hop.start()

                to_partner(zz, xx).start()

    def tile(t, half):
        at = pl.ds(pl.multiple_of(half * HALF, HALF), HALF)

        def pair(q, carry):
            cc = (c + q // 2) % 2
            zz, h = block_of(t, q % 2)
            both = pl.ds(2 * h, 2)
            cg = cols[cc, zz, both, 0:PT, 0:D].reshape(2 * PT, D)
            cb = cols[cc, zz, both, 0:PT, D : 2 * D].reshape(2 * PT, D)
            nt = cols[cc, zz, both, PT:PR, 0:D].astype(F32)
            nj = jnp.concatenate([nt[0, 0:1] + nt[0, 1:2] + nt[0, 2:3], nt[1, 0:1] + nt[1, 1:2] + nt[1, 2:3]], axis=1)
            nh = ni[at, :]
            cross = lax.dot_general(rg[at, :], cg, NT, preferred_element_type=F32)
            coup = lax.dot_general(rb[at, :], cb, NT, preferred_element_type=F32)
            kern = jnp.exp(cross - jnp.concatenate([nh, nh], axis=1) - nj)
            weight = coup * kern
            sw[at, :] += weight[:, 0:D] + weight[:, D : 2 * D]
            acc[at, :] += jnp.dot(weight.astype(BF), cg, preferred_element_type=F32)
            return carry

        lax.fori_loop(0, 4, pair, 0)

    def partner_ready(t):
        for way in (0, 1):
            zz, h = block_of(t, way)
            for i in (0, 1):
                from_partner(zz, 2 * h + i).wait_recv()

    arrivals(1)
    partner_ready(0)
    tile(0, 0)
    arrivals(2)
    partner_ready(1)
    tile(1, 0)
    for s in range(4, 8):
        ready_rows(s)

    def main(j, carry):
        late = j - 2
        t = jnp.where(j < 2, j, 2 + late // 2)
        half = jnp.where(j < 2, 1, jnp.where(j >= 12, 1 - late % 2, late % 2))
        first = jnp.logical_and(j >= 2, late % 2 == 0)

        @pl.when(jnp.logical_and(first, t < 7))
        def _():
            arrivals(t + 1)

        @pl.when(first)
        def _():
            partner_ready(t)

        tile(t, half)
        return carry

    lax.fori_loop(0, 14, main, 0)

    def dist_of(s):
        return (0, 7, 1, 6, 2, 5, 3, 4)[s]

    def part(s):
        at = pl.ds(s * PT, PT)
        total = jnp.sum(sw[at, :], axis=1, keepdims=True)
        return acc[at, :] - total * rg[at, :].astype(F32)

    def t_copy(s):
        k = dist_of(s)
        there = (0, 2, 1, 4, 3, 6, 5, 7)[s]
        return remote(t_send.at[s], t_in.at[there], send_t.at[s], recv_t.at[there], at_y((y + k) % NY))

    for s in range(7, 0, -1):
        t_send[s] = part(s).astype(BF)
    for s in range(7, 0, -1):
        t_copy(s).start()
    total = part(0)
    for s in range(1, 8):
        remote(t_send.at[s], t_in.at[s], send_t.at[s], recv_t.at[s], partner).wait_recv()
        total += t_in[s].astype(F32)

    fg = total * scales[...]
    fg_out[...] = fg
    fgb = fg.astype(BF)
    part_out = jnp.dot(hid_t[...], fgb, preferred_element_type=F32).astype(BF)
    pg = lax.dot_general(fgb, w_out[...], NT, preferred_element_type=F32) * slope[...]
    pb = jnp.sum(pg, axis=0, keepdims=True)
    part_in = jnp.dot(pts_t[...], pg.astype(BF), preferred_element_type=F32).astype(BF)
    tilei = lax.broadcasted_iota(jnp.int32, (16, D), 0)

    def bias_tile(v):
        v_hi, v_mid, v_lo = split3(v)
        z16 = jnp.zeros((16, D), F32)
        return jnp.where(
            tilei == 0, v_hi.astype(F32), jnp.where(tilei == 1, v_mid.astype(F32), jnp.where(tilei == 2, v_lo.astype(F32), z16))
        ).astype(BF)

    for k in range(8):
        g[0, k, 0:PT, :] = part_out[k * PT : (k + 1) * PT, :]
        g[0, k, PT:PR, :] = jnp.zeros((16, D), BF)
        g[1, k, 0:PT, :] = part_in[:, k * D : (k + 1) * D]
        g[1, k, PT:PR, :] = bias_tile(jnp.broadcast_to(pb[:, k * D : (k + 1) * D], (16, D)))

    def at_1(k):
        return dev(jnp.where(c == 0, y, k), jnp.where(c == 0, k, z), x, c)

    def at_2(k):
        return dev(jnp.where(c == 0, k, y), jnp.where(c == 0, z, k), x, c)

    me1 = jnp.where(c == 0, z, y)
    me2 = jnp.where(c == 0, y, z)

    def packed(v):
        b = jnp.sum(v[PT : PT + 8], axis=0, keepdims=True)
        return v[0:PT].astype(BF), bias_tile(jnp.broadcast_to(b, (16, D)))

    half_copy = remote(g.at[1 - c], x_in, send_c.at[0], recv_c.at[0], partner)
    half_copy.start()
    half_copy.wait_recv()

    def combine(k, carry):
        a, b = packed(g[c, k].astype(F32) + x_in[k].astype(F32))
        s1[k, 0:PT] = a
        s1[k, PT:PR] = b
        return carry

    lax.fori_loop(0, 8, combine, 0)

    def line(peers, me, n, src_of, slots, ss, rs):
        def go(k, carry):
            to = (me + k) % n
            remote(src_of(to), slots.at[me], ss.at[k], rs.at[me], peers(to)).start()
            return carry

        def come(k, carry):
            at = (me + k) % n
            remote(src_of(at), slots.at[at], ss.at[k], rs.at[at], peers(at)).wait_recv()
            return carry

        def sent(k, carry):
            to = (me + k) % n
            remote(src_of(to), slots.at[me], ss.at[k], rs.at[me], peers(to)).wait_send()
            return carry

        lax.fori_loop(1, n, go, 0)
        return lambda: lax.fori_loop(1, n, come, 0), lambda: lax.fori_loop(1, n, sent, 0)

    come, sent1 = line(at_1, me1, 8, lambda k: s1.at[k], in1, send_1, recv_1)
    in1[me1] = s1[me1]
    come()
    tot = in1[0].astype(F32)
    for k in range(1, 8):
        tot += in1[k].astype(F32)
    a, b = packed(tot)
    in2[me2, 0:PT] = a
    in2[me2, PT:PR] = b
    come, sent2 = line(at_2, me2, 8, lambda k: in2.at[me2], in2, send_2, recv_2)
    come()
    tot = in2[0].astype(F32)
    for k in range(1, 8):
        tot += in2[k].astype(F32)
    a, b = packed(tot)
    in3[x, 0:PT] = a
    in3[x, PT:PR] = b
    come, sent3 = line(at_x, x, NX, lambda k: in3.at[x], in3, send_3, recv_3)
    come()
    tot = in3[0].astype(F32)
    for k in range(1, NX):
        tot += in3[k].astype(F32)
    a, b = packed(tot)
    fin[c, me1, 0:PT] = a
    fin[c, me1, PT:PR] = b
    come, sent4 = line(at_1, me1, 8, lambda k: fin.at[c, me1], fin.at[c], send_4, recv_4)
    come()
    out_copy = remote(fin.at[c], fin.at[c], send_c.at[1], recv_c.at[1], partner)
    out_copy.start()
    remote(fin.at[1 - c], fin.at[1 - c], send_c.at[1], recv_c.at[1], partner).wait_recv()

    factor = 1.0 / 256.0
    for k in range(8):
        go_out[k * PT : (k + 1) * PT, :] = factor * fin[0, k, 0:PT].astype(F32)
        gi_out[:, k * D : (k + 1) * D] = factor * fin[1, k, 0:PT].astype(F32)
        bt = fin[1, k, PT:PR].astype(F32)
        gb_out[k : k + 1, :] = factor * (bt[0:1] + bt[1:2] + bt[2:3])

    for k in (1, 3, 2):
        x_copy(k).wait_send()
    for k in range(1, 8):
        y_copy(k).wait_send()
        t_copy(k).wait_send()

    def z_sent(i, carry):
        zz, xx = i // NX, i % NX
        back = (z + NZ - zz) % NZ
        ahead = (zz + NZ - z) % NZ

        @pl.when(jnp.logical_or(back < 3, jnp.logical_and(back == 3, xx < 2)))
        def _():
            z_right(zz, xx).wait_send()

        @pl.when(jnp.logical_or(ahead < 3, jnp.logical_and(ahead == 3, xx >= 2)))
        def _():
            z_left(zz, xx).wait_send()

        to_partner(zz, xx).wait_send()
        return carry

    lax.fori_loop(0, NZ * NX, z_sent, 0)
    half_copy.wait_send()
    out_copy.wait_send()
    sent1()
    sent2()
    sent3()
    sent4()


def local(points, w_in, b_in, w_out, scales, left, right):
    vmem = pl.BlockSpec(memory_space=pltpu.VMEM)
    dma = pltpu.SemaphoreType.DMA
    piece = (PR, D)
    fg, gi, gb, go = pl.pallas_call(
        body,
        out_shape=[
            jax.ShapeDtypeStruct((PT, D), F32),
            jax.ShapeDtypeStruct((D, HID), F32),
            jax.ShapeDtypeStruct((8, D), F32),
            jax.ShapeDtypeStruct((HID, D), F32),
        ],
        in_specs=[vmem] * 7,
        out_specs=[vmem] * 4,
        scratch_shapes=[
            pltpu.VMEM((PT, HID), F32),
            pltpu.VMEM((HID, PT), BF),
            pltpu.VMEM((D, PT), BF),
            pltpu.VMEM((NY, PR, 2 * D), BF),
            pltpu.VMEM((NC, NZ, NX, PR, 2 * D), BF),
            pltpu.VMEM((NY * PT, D), BF),
            pltpu.VMEM((NY * PT, D), BF),
            pltpu.VMEM((NY * PT, D), F32),
            pltpu.VMEM((NY * PT, D), F32),
            pltpu.VMEM((NY * PT, D), F32),
            pltpu.VMEM((NY, PT, D), BF),
            pltpu.VMEM((NY, PT, D), BF),
            pltpu.VMEM((2, 8) + piece, BF),
            pltpu.VMEM((8,) + piece, BF),
            pltpu.VMEM((8,) + piece, BF),
            pltpu.VMEM((8,) + piece, BF),
            pltpu.VMEM((8,) + piece, BF),
            pltpu.VMEM((NX,) + piece, BF),
            pltpu.VMEM((2, 8) + piece, BF),
            dma((8,)), dma((8,)), dma((4,)), dma((4,)),
            dma((2, NZ, NX)), dma((NZ, NX)), dma((NZ, NX)), dma((NZ, NX)),
            dma((8,)), dma((8,)), dma((2,)), dma((2,)),
            dma((8,)), dma((8,)), dma((8,)), dma((8,)), dma((4,)), dma((4,)), dma((8,)), dma((8,)),
        ],
        compiler_params=pltpu.CompilerParams(collective_id=0, has_side_effects=True),
        name="gp_grad",
    )(points, w_in, b_in.reshape(1, HID), w_out, scales.reshape(1, D), left, right)
    return fg, gi, gb.reshape(HID), go


def solution(mesh):
    placed = (
        P(("blk", "row"), None),
        P(),
        P(),
        P(),
        P(),
        P(("blk", "row"), None),
        P(("blk", "row"), None),
    )
    return jax.shard_map(
        local,
        mesh=mesh,
        in_specs=placed,
        out_specs=(P(("blk", "row"), None), P(), P(), P()),
        check_vma=False,
    )
```

```python
import jax
import jax.numpy as jnp
from jax import lax
from jax.experimental import pallas as pl
from jax.experimental.pallas import tpu as pltpu
from jax.sharding import PartitionSpec as P

NX, NY, NZ, NC = 4, 8, 8, 2
PT = 128
PR = 144
D = 128
HID = 1024
HALF = 512
BF = jnp.bfloat16
F32 = jnp.float32
MESH = pl.DeviceIdType.MESH
NT = (((1,), (1,)), ((), ()))


def split3(v):
    hi = v.astype(BF)
    rest = v - hi.astype(F32)
    mid = rest.astype(BF)
    lo = (rest - mid.astype(F32)).astype(BF)
    return hi, mid, lo


def body(
    points, w_in, b_in, w_out, scales, left, right,
    fg_out, fin_out,
    slope, hid_t, pts_t, rows, cols, rg, rb, ni, acc, sw, t_send, t_in,
    g, x_in, s1, in1, in2, in3, fin,
    send_y, recv_y, send_x, send_z, recv_a, send_p, recv_p,
    send_t, recv_t, send_c, recv_c, send_1, recv_1, send_2, recv_2, send_3, recv_3, send_4, recv_4,
):
    blk = lax.axis_index("blk")
    row = lax.axis_index("row")
    y_lo = blk // (NX * NZ)
    z = (blk // NX) % NZ
    x = blk % NX
    c = row % 2
    y = (row // 2) * 2 + y_lo

    def dev(y_, z_, x_, c_):
        return (((y_ % 2) * NZ + z_) * NX + x_, (y_ // 2) * 2 + c_)

    def at_y(k):
        return dev(k, z, x, c)

    def at_z(k):
        return dev(y, k, x, c)

    def at_x(k):
        return dev(y, z, k, c)

    partner = dev(y, z, x, 1 - c)
    nxt = at_z((z + 1) % NZ)
    prv = at_z((z + NZ - 1) % NZ)

    def remote(src, dst, ss, rs, device):
        return pltpu.make_async_remote_copy(
            src_ref=src, dst_ref=dst, send_sem=ss, recv_sem=rs, device_id=device, device_id_type=MESH
        )

    bar = pltpu.get_barrier_semaphore()

    def hello(device):
        pl.semaphore_signal(bar, inc=1, device_id=device, device_id_type=MESH)

    hello(partner)
    for k in range(1, NX):
        hello(at_x((x + k) % NX))
    for k in range(1, NZ):
        hello(at_z((z + k) % NZ))
    for k in range(1, NY):
        hello(at_y((y + k) % NY))

    pts = points[...]
    pre = jnp.dot(pts, w_in[...], preferred_element_type=F32) + b_in[...]
    sig = jax.nn.sigmoid(pre)
    hidden = (pre * sig).astype(BF)
    feats = jnp.dot(hidden, w_out[...], preferred_element_type=F32)
    scaled = (feats * scales[...]).astype(BF)
    sf = scaled.astype(F32)
    sq = sf * sf
    sq_hi = sq.astype(BF)
    sq_lo = (sq - sq_hi.astype(F32)).astype(BF)
    ones = jnp.full((16, D), 0.5, BF)
    norm = lax.dot_general(ones, sq_hi, NT, preferred_element_type=F32) + lax.dot_general(
        ones, sq_lo, NT, preferred_element_type=F32
    )
    hi, mid, lo = split3(norm)
    which = lax.broadcasted_iota(jnp.int32, (16, D), 0)
    zero = jnp.zeros((16, D), F32)
    tail = jnp.where(
        which == 0, hi.astype(F32), jnp.where(which == 1, mid.astype(F32), jnp.where(which == 2, lo.astype(F32), zero))
    ).astype(BF)
    mine = cols.at[c, z, x]
    mine[0:PT, 0:D] = scaled
    mine[0:PT, D : 2 * D] = jnp.concatenate([left[...].astype(F32), right[...].astype(F32)], axis=0).T.astype(BF)
    mine[PT:PR, 0:D] = tail
    mine[PT:PR, D : 2 * D] = jnp.zeros((16, D), BF)

    pl.semaphore_wait(bar, 1 + (NX - 1) + (NZ - 1) + (NY - 1))

    def slot_y(k):
        return jnp.where(k == 4, 7, jnp.where(k == 0, 0, jnp.where(k > 4, 2 * (8 - k) - 1, 2 * k)))

    def piece(zz, xx):
        return cols.at[c, zz, xx]

    def arrival(zz, xx):
        return remote(piece(zz, xx), piece(zz, xx), send_p.at[zz, xx], recv_a.at[zz, xx], partner)

    def z_right(zz, xx):
        return remote(piece(zz, xx), piece(zz, xx), send_z.at[0, zz, xx], recv_a.at[zz, xx], nxt)

    def z_left(zz, xx):
        return remote(piece(zz, xx), piece(zz, xx), send_z.at[1, zz, xx], recv_a.at[zz, xx], prv)

    def z_direct(k):
        return remote(mine, mine, send_z.at[0, k, 0], recv_a.at[z, x], at_z((z + k) % NZ))

    def x_copy(zz, k):
        return remote(piece(zz, x), piece(zz, x), send_x.at[zz, k], recv_a.at[zz, x], at_x((x + k) % NX))

    def to_partner(zz, xx):
        return remote(piece(zz, xx), piece(zz, xx), send_p.at[zz, xx], recv_p.at[zz, xx], partner)

    def from_partner(zz, xx):
        return remote(cols.at[1 - c, zz, xx], cols.at[1 - c, zz, xx], send_p.at[zz, xx], recv_p.at[zz, xx], partner)

    def y_copy(k):
        return remote(mine, rows.at[slot_y((8 - k) % 8)], send_y.at[k], recv_y.at[slot_y((8 - k) % 8)], at_y((y + k) % NY))

    def y_from(s):
        return remote(mine, rows.at[s], send_y.at[0], recv_y.at[s], partner)

    @pl.when(c == 0)
    def _():
        z_right(z, x).start()
        z_left(z, x).start()

    for k in (1, 3, 2):
        x_copy(z, k).start()
    to_partner(z, x).start()
    for k in (1, 7, 2, 6):
        y_copy(k).start()

    @pl.when(c == 1)
    def _():
        for k in (1, 7, 2, 6, 3, 5, 4):
            z_direct(k).start()

    rows[0] = mine[...]
    slope[...] = sig * (1.0 + pre * (1.0 - sig))
    hid_t[...] = hidden.astype(F32).T.astype(BF)
    pts_t[...] = pts.astype(F32).T.astype(BF)
    acc[...] = jnp.zeros_like(acc)
    sw[...] = jnp.zeros_like(sw)

    for k in (1, 3, 2):
        xx = (x + k) % NX
        arrival(z, xx).wait_recv()

        @pl.when(c == 0)
        def _():
            z_right(z, xx).start()
            z_left(z, xx).start()

        to_partner(z, xx).start()

    for k in (3, 5, 4):
        y_copy(k).start()

    def spread(zz):
        arrival(zz, x).wait_recv()
        for k in (1, 3, 2):
            x_copy(zz, k).start()
        to_partner(zz, x).start()

    @pl.when(c == 1)
    def _():
        spread((z + NZ - 1) % NZ)
        spread((z + 1) % NZ)

    def ready_rows(s):
        if s > 0:
            y_from(s).wait_recv()
        gg = rows[s, 0:PT, 0:D]
        ab = rows[s, 0:PT, D : 2 * D].astype(F32)
        at = pl.ds(s * PT, PT)
        rg[at, :] = gg
        rb[at, :] = pltpu.roll(ab, 64, 1).astype(BF)
        gf = gg.astype(F32)
        ni[at, :] = jnp.broadcast_to(0.5 * jnp.sum(gf * gf, axis=1, keepdims=True), (PT, D))

    for s in range(4):
        ready_rows(s)

    def block_of(t, way):
        edge = jnp.logical_or(t == 0, t == 7)
        dist = (t + 1) // 2
        zz = jnp.where(way == 0, (z + NZ - dist) % NZ, (z + dist) % NZ)
        h = jnp.where(edge, way, (t + 1) % 2)
        return zz, h

    def arrivals(t):
        dist = (t + 1) // 2

        @pl.when(c == 0)
        def _():
            for way in (0, 1):
                zz, h = block_of(t, way)
                on = jnp.logical_or(dist + 1 < 4, jnp.logical_and(dist == 3, h == way))
                for i in (0, 1):
                    xx = 2 * h + i
                    arrival(zz, xx).wait_recv()

                    @pl.when(on)
                    def _():
                        if way == 0:
                            z_right(zz, xx).start()
                        else:
                            z_left(zz, xx).start()

                    to_partner(zz, xx).start()

        @pl.when(c == 1)
        def _():
            @pl.when(t < 4)
            def _():
                spread((z + NZ - (t + 1)) % NZ)

            @pl.when(t < 3)
            def _():
                spread((z + t + 1) % NZ)

            for way in (0, 1):
                zz, h = block_of(t, way)
                for i in (0, 1):
                    xx = 2 * h + i

                    @pl.when(xx != x)
                    def _():
                        arrival(zz, xx).wait_recv()
                        to_partner(zz, xx).start()

    def tile(t, half):
        at = pl.ds(pl.multiple_of(half * HALF, HALF), HALF)
        nh = ni[at, :]
        nh2 = jnp.concatenate([nh, nh], axis=1)

        def quad(q, carry):
            cc = (c + q) % 2
            weights, gs = [], []
            for way in (0, 1):
                zz, h = block_of(t, way)
                both = pl.ds(2 * h, 2)
                cg = cols[cc, zz, both, 0:PT, 0:D].reshape(2 * PT, D)
                cb = cols[cc, zz, both, 0:PT, D : 2 * D].reshape(2 * PT, D)
                nt = cols[cc, zz, both, PT:PR, 0:D].astype(F32)
                nj = jnp.concatenate([nt[0, 0:1] + nt[0, 1:2] + nt[0, 2:3], nt[1, 0:1] + nt[1, 1:2] + nt[1, 2:3]], axis=1)
                cross = lax.dot_general(rg[at, :], cg, NT, preferred_element_type=F32)
                coup = lax.dot_general(rb[at, :], cb, NT, preferred_element_type=F32)
                weights.append(coup * jnp.exp(cross - nh2 - nj))
                gs.append(cg)
            v, w = weights
            sw[at, :] += (v[:, 0:D] + v[:, D : 2 * D]) + (w[:, 0:D] + w[:, D : 2 * D])
            acc[at, :] += jnp.dot(
                jnp.concatenate([v.astype(BF), w.astype(BF)], axis=1), jnp.concatenate(gs, axis=0), preferred_element_type=F32
            )
            return carry

        lax.fori_loop(0, 2, quad, 0, unroll=2)

    def partner_ready(t):
        for way in (0, 1):
            zz, h = block_of(t, way)
            for i in (0, 1):
                from_partner(zz, 2 * h + i).wait_recv()

    def dist_of(s):
        return (0, 7, 1, 6, 2, 5, 3, 4)[s]

    def part(s):
        at = pl.ds(s * PT, PT)
        total = jnp.sum(sw[at, :], axis=1, keepdims=True)
        return acc[at, :] - total * rg[at, :].astype(F32)

    def t_copy(s):
        k = dist_of(s)
        there = (0, 2, 1, 4, 3, 6, 5, 7)[s]
        return remote(t_send.at[s], t_in.at[there], send_t.at[s], recv_t.at[there], at_y((y + k) % NY))

    def main(j, carry):
        t = jnp.where(j < 3, j, jnp.where(j < 6, j - 3, jnp.where(j < 12, 3 + (j - 6) // 2, 6 + (j - 12) % 2)))
        half = jnp.where(j < 3, 0, jnp.where(j < 6, 1, jnp.where(j < 12, j % 2, 1 - (j - 12) // 2)))
        even = j % 2 == 0
        first = jnp.logical_or(j < 3, jnp.logical_or(jnp.logical_and(jnp.logical_and(j >= 6, j < 12), even), jnp.logical_or(j == 12, j == 13)))

        @pl.when(j == 3)
        def _():
            for s in range(4, 8):
                ready_rows(s)

        @pl.when(j == 14)
        def _():
            for s in (7, 6, 5, 4):
                t_send[s] = part(s).astype(BF)
            for s in (7, 6, 5, 4):
                t_copy(s).start()

        @pl.when(first)
        def _():
            partner_ready(t)

        tile(t, half)
        later = jnp.logical_and(even, jnp.logical_and(j >= 4, j <= 10))

        @pl.when(jnp.logical_or(j < 3, later))
        def _():
            arrivals(jnp.where(j < 3, j + 1, j // 2 + 2))

        return carry

    lax.fori_loop(0, 16, main, 0)

    for s in (3, 2, 1):
        t_send[s] = part(s).astype(BF)
    for s in (3, 2, 1):
        t_copy(s).start()
    total = part(0)
    for s in range(1, 8):
        remote(t_send.at[s], t_in.at[s], send_t.at[s], recv_t.at[s], partner).wait_recv()
        total += t_in[s].astype(F32)

    fg = total * scales[...]
    fg_out[...] = fg
    fgb = fg.astype(BF)
    part_out = jnp.dot(hid_t[...], fgb, preferred_element_type=F32).astype(BF)
    pg = lax.dot_general(fgb, w_out[...], NT, preferred_element_type=F32) * slope[...]
    pb = jnp.sum(pg, axis=0, keepdims=True)
    part_in = jnp.dot(pts_t[...], pg.astype(BF), preferred_element_type=F32).astype(BF)
    tilei = lax.broadcasted_iota(jnp.int32, (16, D), 0)

    def bias_tile(v):
        v_hi, v_mid, v_lo = split3(v)
        z16 = jnp.zeros((16, D), F32)
        return jnp.where(
            tilei == 0, v_hi.astype(F32), jnp.where(tilei == 1, v_mid.astype(F32), jnp.where(tilei == 2, v_lo.astype(F32), z16))
        ).astype(BF)

    for k in range(8):
        g[0, k, 0:PT, :] = part_out[k * PT : (k + 1) * PT, :]
        g[0, k, PT:PR, :] = jnp.zeros((16, D), BF)
        g[1, k, 0:PT, :] = part_in[:, k * D : (k + 1) * D]
        g[1, k, PT:PR, :] = bias_tile(jnp.broadcast_to(pb[:, k * D : (k + 1) * D], (16, D)))

    def at_1(k):
        return dev(jnp.where(c == 0, y, k), jnp.where(c == 0, k, z), x, c)

    def at_2(k):
        return dev(jnp.where(c == 0, k, y), jnp.where(c == 0, z, k), x, c)

    me1 = jnp.where(c == 0, z, y)
    me2 = jnp.where(c == 0, y, z)

    def packed(v):
        b = jnp.sum(v[PT : PT + 8], axis=0, keepdims=True)
        return v[0:PT].astype(BF), bias_tile(jnp.broadcast_to(b, (16, D)))

    half_copy = remote(g.at[1 - c], x_in, send_c.at[0], recv_c.at[0], partner)
    half_copy.start()
    half_copy.wait_recv()

    def combine(k, carry):
        a, b = packed(g[c, k].astype(F32) + x_in[k].astype(F32))
        s1[k, 0:PT] = a
        s1[k, PT:PR] = b
        return carry

    lax.fori_loop(0, 8, combine, 0)

    def line(peers, me, n, src_of, slots, ss, rs):
        def go(k, carry):
            to = (me + k) % n
            remote(src_of(to), slots.at[me], ss.at[k], rs.at[me], peers(to)).start()
            return carry

        def come(k, carry):
            at = (me + k) % n
            remote(src_of(at), slots.at[at], ss.at[k], rs.at[at], peers(at)).wait_recv()
            return carry

        def sent(k, carry):
            to = (me + k) % n
            remote(src_of(to), slots.at[me], ss.at[k], rs.at[me], peers(to)).wait_send()
            return carry

        lax.fori_loop(1, n, go, 0)
        return lambda: lax.fori_loop(1, n, come, 0), lambda: lax.fori_loop(1, n, sent, 0)

    come, sent1 = line(at_1, me1, 8, lambda k: s1.at[k], in1, send_1, recv_1)
    in1[me1] = s1[me1]
    come()
    tot = in1[0].astype(F32)
    for k in range(1, 8):
        tot += in1[k].astype(F32)
    a, b = packed(tot)
    in2[me2, 0:PT] = a
    in2[me2, PT:PR] = b
    come, sent2 = line(at_2, me2, 8, lambda k: in2.at[me2], in2, send_2, recv_2)
    come()
    tot = in2[0].astype(F32)
    for k in range(1, 8):
        tot += in2[k].astype(F32)
    a, b = packed(tot)
    in3[x, 0:PT] = a
    in3[x, PT:PR] = b
    come, sent3 = line(at_x, x, NX, lambda k: in3.at[x], in3, send_3, recv_3)
    come()
    tot = in3[0].astype(F32)
    for k in range(1, NX):
        tot += in3[k].astype(F32)
    a, b = packed(tot)
    fin[c, me1, 0:PT] = a
    fin[c, me1, PT:PR] = b
    come, sent4 = line(at_1, me1, 8, lambda k: fin.at[c, me1], fin.at[c], send_4, recv_4)
    come()
    out_copy = remote(fin.at[c], fin.at[c], send_c.at[1], recv_c.at[1], partner)
    out_copy.start()
    remote(fin.at[1 - c], fin.at[1 - c], send_c.at[1], recv_c.at[1], partner).wait_recv()

    fin_out[...] = fin[...]

    for k in (1, 3, 2):
        x_copy(z, k).wait_send()
    for k in range(1, 8):
        y_copy(k).wait_send()
        t_copy(k).wait_send()

    def sent(i, carry):
        zz, xx = i // NX, i % NX
        back = (z + NZ - zz) % NZ
        ahead = (zz + NZ - z) % NZ

        @pl.when(c == 0)
        def _():
            @pl.when(jnp.logical_or(back < 3, jnp.logical_and(back == 3, xx < 2)))
            def _():
                z_right(zz, xx).wait_send()

            @pl.when(jnp.logical_or(ahead < 3, jnp.logical_and(ahead == 3, xx >= 2)))
            def _():
                z_left(zz, xx).wait_send()

        to_partner(zz, xx).wait_send()
        return carry

    lax.fori_loop(0, NZ * NX, sent, 0)

    @pl.when(c == 1)
    def _():
        for k in range(1, NZ):
            z_direct(k).wait_send()
            for m in (1, 3, 2):
                x_copy((z + k) % NZ, m).wait_send()

    half_copy.wait_send()
    out_copy.wait_send()
    sent1()
    sent2()
    sent3()
    sent4()


def finish(fg_in, fin, fg_out, gi_out, gb_out, go_out):
    factor = 1.0 / 256.0
    fg_out[...] = fg_in[...]
    for k in range(8):
        go_out[k * PT : (k + 1) * PT, :] = factor * fin[0, k, 0:PT].astype(F32)
        gi_out[:, k * D : (k + 1) * D] = factor * fin[1, k, 0:PT].astype(F32)
        bt = fin[1, k, PT:PR].astype(F32)
        gb_out[k : k + 1, :] = factor * (bt[0:1] + bt[1:2] + bt[2:3])


def local(points, w_in, b_in, w_out, scales, left, right):
    vmem = pl.BlockSpec(memory_space=pltpu.VMEM)
    dma = pltpu.SemaphoreType.DMA
    piece = (PR, D)
    fg, sums = pl.pallas_call(
        body,
        out_shape=[
            jax.ShapeDtypeStruct((PT, D), F32),
            jax.ShapeDtypeStruct((2, 8) + piece, BF),
        ],
        in_specs=[vmem] * 7,
        out_specs=[vmem] * 2,
        scratch_shapes=[
            pltpu.VMEM((PT, HID), F32),
            pltpu.VMEM((HID, PT), BF),
            pltpu.VMEM((D, PT), BF),
            pltpu.VMEM((NY, PR, 2 * D), BF),
            pltpu.VMEM((NC, NZ, NX, PR, 2 * D), BF),
            pltpu.VMEM((NY * PT, D), BF),
            pltpu.VMEM((NY * PT, D), BF),
            pltpu.VMEM((NY * PT, D), F32),
            pltpu.VMEM((NY * PT, D), F32),
            pltpu.VMEM((NY * PT, D), F32),
            pltpu.VMEM((NY, PT, D), BF),
            pltpu.VMEM((NY, PT, D), BF),
            pltpu.VMEM((2, 8) + piece, BF),
            pltpu.VMEM((8,) + piece, BF),
            pltpu.VMEM((8,) + piece, BF),
            pltpu.VMEM((8,) + piece, BF),
            pltpu.VMEM((8,) + piece, BF),
            pltpu.VMEM((NX,) + piece, BF),
            pltpu.VMEM((2, 8) + piece, BF),
            dma((8,)), dma((8,)), dma((NZ, NX)),
            dma((2, NZ, NX)), dma((NZ, NX)), dma((NZ, NX)), dma((NZ, NX)),
            dma((8,)), dma((8,)), dma((2,)), dma((2,)),
            dma((8,)), dma((8,)), dma((8,)), dma((8,)), dma((4,)), dma((4,)), dma((8,)), dma((8,)),
        ],
        compiler_params=pltpu.CompilerParams(collective_id=0, has_side_effects=True),
        name="gp_grad",
    )(points, w_in, b_in.reshape(1, HID), w_out, scales.reshape(1, D), left.T, right.T)
    fg, gi, gb, go = pl.pallas_call(
        finish,
        out_shape=[
            jax.ShapeDtypeStruct((PT, D), F32),
            jax.ShapeDtypeStruct((D, HID), F32),
            jax.ShapeDtypeStruct((8, D), F32),
            jax.ShapeDtypeStruct((HID, D), F32),
        ],
        in_specs=[vmem] * 2,
        out_specs=[vmem] * 4,
        name="finish",
    )(fg, sums)
    return fg, gi, gb.reshape(HID), go


def solution(mesh):
    placed = (
        P(("blk", "row"), None),
        P(),
        P(),
        P(),
        P(),
        P(("blk", "row"), None),
        P(("blk", "row"), None),
    )
    return jax.shard_map(
        local,
        mesh=mesh,
        in_specs=placed,
        out_specs=(P(("blk", "row"), None), P(), P(), P()),
        check_vma=False,
    )
```

```python
import jax
import jax.numpy as jnp
from jax import lax
from jax.experimental import pallas as pl
from jax.experimental.pallas import tpu as pltpu
from jax.sharding import PartitionSpec as P

NX, NY, NZ, NC = 4, 8, 8, 2
PT = 128
PR = 144
D = 128
HID = 1024
HALF = 512
BF = jnp.bfloat16
F32 = jnp.float32
MESH = pl.DeviceIdType.MESH
NT = (((1,), (1,)), ((), ()))


def split3(v):
    hi = v.astype(BF)
    rest = v - hi.astype(F32)
    mid = rest.astype(BF)
    lo = (rest - mid.astype(F32)).astype(BF)
    return hi, mid, lo


def body(
    points_hbm, w_in_hbm, b_in, w_out_hbm, scales, left_hbm, right_hbm,
    fg_out, fin_out,
    points, w_in, w_out, left, right, fg_buf,
    slope, hid_t, pts_t, rows, cols, rg, rb, ni, acc, sw, t_send, t_in,
    g, x_in, s1, in1, in2, in3, fin,
    load, store, send_y, recv_y, send_x, send_d, send_z, recv_a, recv_r, send_p, recv_p,
    send_t, recv_t, send_c, recv_c, send_1, recv_1, send_2, recv_2, send_3, recv_3, send_4, recv_4,
):
    blk = lax.axis_index("blk")
    row = lax.axis_index("row")
    y_lo = blk // (NX * NZ)
    z = (blk // NX) % NZ
    x = blk % NX
    c = row % 2
    y = (row // 2) * 2 + y_lo

    def dev(y_, z_, x_, c_):
        return (((y_ % 2) * NZ + z_) * NX + x_, (y_ // 2) * 2 + c_)

    def at_y(k):
        return dev(k, z, x, c)

    def at_z(k):
        return dev(y, k, x, c)

    def at_x(k):
        return dev(y, z, k, c)

    partner = dev(y, z, x, 1 - c)
    nxt = at_z((z + 1) % NZ)
    prv = at_z((z + NZ - 1) % NZ)

    def remote(src, dst, ss, rs, device):
        return pltpu.make_async_remote_copy(
            src_ref=src, dst_ref=dst, send_sem=ss, recv_sem=rs, device_id=device, device_id_type=MESH
        )

    loads = [
        pltpu.make_async_copy(src, dst, load.at[k])
        for k, (src, dst) in enumerate(
            ((points_hbm, points), (w_in_hbm, w_in), (w_out_hbm, w_out), (left_hbm, left), (right_hbm, right))
        )
    ]
    for copy in loads:
        copy.start()

    bar = pltpu.get_barrier_semaphore()

    def hello(device):
        pl.semaphore_signal(bar, inc=1, device_id=device, device_id_type=MESH)

    hello(partner)
    for k in range(1, NX):
        hello(at_x((x + k) % NX))
    for k in range(1, NZ):
        hello(at_z((z + k) % NZ))
    for k in range(1, NY):
        hello(at_y((y + k) % NY))

    loads[0].wait()
    loads[1].wait()
    pts = points[...]
    pre = jnp.dot(pts, w_in[...], preferred_element_type=F32) + b_in[...]
    sig = jax.nn.sigmoid(pre)
    hidden = (pre * sig).astype(BF)
    loads[2].wait()
    feats = jnp.dot(hidden, w_out[...], preferred_element_type=F32)
    scaled = (feats * scales[...]).astype(BF)
    sf = scaled.astype(F32)
    sq = sf * sf
    sq_hi = sq.astype(BF)
    sq_lo = (sq - sq_hi.astype(F32)).astype(BF)
    ones = jnp.full((16, D), 0.5, BF)
    norm = lax.dot_general(ones, sq_hi, NT, preferred_element_type=F32) + lax.dot_general(
        ones, sq_lo, NT, preferred_element_type=F32
    )
    hi, mid, lo = split3(norm)
    which = lax.broadcasted_iota(jnp.int32, (16, D), 0)
    zero = jnp.zeros((16, D), F32)
    tail = jnp.where(
        which == 0, hi.astype(F32), jnp.where(which == 1, mid.astype(F32), jnp.where(which == 2, lo.astype(F32), zero))
    ).astype(BF)
    mine = cols.at[c, z, x]
    mine[0:PT, 0:D] = scaled
    loads[3].wait()
    loads[4].wait()
    mine[0:PT, D : 2 * D] = jnp.concatenate([left[...].astype(F32), right[...].astype(F32)], axis=0).T.astype(BF)
    mine[PT:PR, 0:D] = tail
    mine[PT:PR, D : 2 * D] = jnp.zeros((16, D), BF)

    pl.semaphore_wait(bar, 1 + (NX - 1) + (NZ - 1) + (NY - 1))

    def slot_y(k):
        return jnp.where(k == 4, 7, jnp.where(k == 0, 0, jnp.where(k > 4, 2 * (8 - k) - 1, 2 * k)))

    def piece(zz, xx):
        return cols.at[c, zz, xx]

    def duo(zz, h):
        return cols.at[c, zz, pl.ds(2 * h, 2)]

    def arrival(zz, xx):
        return remote(piece(zz, xx), piece(zz, xx), send_x.at[0, 0], recv_a.at[zz, xx], partner)

    def z_right(zz, h):
        return remote(duo(zz, h), duo(zz, h), send_z.at[0, zz, h], recv_r.at[zz, h], nxt)

    def z_left(zz, h):
        return remote(duo(zz, h), duo(zz, h), send_z.at[1, zz, h], recv_r.at[zz, h], prv)

    def z_direct(k):
        return remote(mine, mine, send_d.at[k], recv_a.at[z, x], at_z((z + k) % NZ))

    def x_copy(zz, k):
        return remote(piece(zz, x), piece(zz, x), send_x.at[zz, k], recv_a.at[zz, x], at_x((x + k) % NX))

    def to_partner(zz, h):
        return remote(duo(zz, h), duo(zz, h), send_p.at[zz, h], recv_p.at[zz, h], partner)

    def from_partner(zz, h):
        there = cols.at[1 - c, zz, pl.ds(2 * h, 2)]
        return remote(there, there, send_p.at[zz, h], recv_p.at[zz, h], partner)

    def y_copy(k):
        return remote(mine, rows.at[slot_y((8 - k) % 8)], send_y.at[k], recv_y.at[slot_y((8 - k) % 8)], at_y((y + k) % NY))

    def y_from(s):
        return remote(mine, rows.at[s], send_y.at[0], recv_y.at[s], partner)

    def ready_rows(s):
        if s > 0:
            y_from(s).wait_recv()
        gg = rows[s, 0:PT, 0:D]
        ab = rows[s, 0:PT, D : 2 * D].astype(F32)
        at = pl.ds(s * PT, PT)
        rg[at, :] = gg
        rb[at, :] = pltpu.roll(ab, 64, 1).astype(BF)
        gf = gg.astype(F32)
        ni[at, :] = jnp.broadcast_to(0.5 * jnp.sum(gf * gf, axis=1, keepdims=True), (PT, D))

    @pl.when(c == 0)
    def _():
        for k in (1, 3, 2):
            x_copy(z, k).start()

    for k in (1, 7, 2, 6):
        y_copy(k).start()

    @pl.when(c == 1)
    def _():
        for k in (1, 7, 2, 6, 3, 5, 4):
            z_direct(k).start()

    rows[0] = mine[...]
    ready_rows(0)
    slope[...] = sig * (1.0 + pre * (1.0 - sig))
    hid_t[...] = hidden.astype(F32).T.astype(BF)
    pts_t[...] = pts.astype(F32).T.astype(BF)
    acc[...] = jnp.zeros_like(acc)
    sw[...] = jnp.zeros_like(sw)

    @pl.when(c == 1)
    def _():
        for k in (1, 3, 2):
            x_copy(z, k).start()

    own = x // 2

    def ready_duo(h):
        @pl.when(c == 0)
        def _():
            z_right(z, h).start()
            z_left(z, h).start()

        to_partner(z, h).start()

    arrival(z, x + 1 - 2 * (x % 2)).wait_recv()
    ready_duo(own)
    for i in (0, 1):
        arrival(z, 2 * (1 - own) + i).wait_recv()
    ready_duo(1 - own)

    for k in (3, 5, 4):
        y_copy(k).start()

    def spread(zz):
        arrival(zz, x).wait_recv()
        for k in (1, 3, 2):
            x_copy(zz, k).start()

    @pl.when(c == 1)
    def _():
        spread((z + NZ - 1) % NZ)
        spread((z + 1) % NZ)

    for s in range(1, 4):
        ready_rows(s)

    def block_of(t, way):
        edge = jnp.logical_or(t == 0, t == 7)
        dist = (t + 1) // 2
        zz = jnp.where(way == 0, (z + NZ - dist) % NZ, (z + dist) % NZ)
        h = jnp.where(edge, way, (t + 1) % 2)
        return zz, h

    def arrivals(t):
        dist = (t + 1) // 2

        @pl.when(c == 0)
        def _():
            for way in (0, 1):
                zz, h = block_of(t, way)
                on = jnp.logical_or(dist + 1 < 4, jnp.logical_and(dist == 3, h == way))
                hop = z_right(zz, h) if way == 0 else z_left(zz, h)
                hop.wait_recv()

                @pl.when(on)
                def _():
                    hop.start()

                to_partner(zz, h).start()

        @pl.when(c == 1)
        def _():
            @pl.when(t < 4)
            def _():
                spread((z + NZ - (t + 1)) % NZ)

            @pl.when(t < 3)
            def _():
                spread((z + t + 1) % NZ)

            for way in (0, 1):
                zz, h = block_of(t, way)
                for i in (0, 1):
                    xx = 2 * h + i

                    @pl.when(xx != x)
                    def _():
                        arrival(zz, xx).wait_recv()

                to_partner(zz, h).start()

    def tile(t, half):
        at = pl.ds(pl.multiple_of(half * HALF, HALF), HALF)
        nh = ni[at, :]
        nh2 = jnp.concatenate([nh, nh], axis=1)

        def quad(q, carry):
            cc = (c + q) % 2
            weights, gs = [], []
            for way in (0, 1):
                zz, h = block_of(t, way)
                both = pl.ds(2 * h, 2)
                cg = cols[cc, zz, both, 0:PT, 0:D].reshape(2 * PT, D)
                cb = cols[cc, zz, both, 0:PT, D : 2 * D].reshape(2 * PT, D)
                nt = cols[cc, zz, both, PT:PR, 0:D].astype(F32)
                nj = jnp.concatenate([nt[0, 0:1] + nt[0, 1:2] + nt[0, 2:3], nt[1, 0:1] + nt[1, 1:2] + nt[1, 2:3]], axis=1)
                cross = lax.dot_general(rg[at, :], cg, NT, preferred_element_type=F32)
                coup = lax.dot_general(rb[at, :], cb, NT, preferred_element_type=F32)
                weights.append(coup * jnp.exp(cross - nh2 - nj))
                gs.append(cg)
            v, w = weights
            sw[at, :] += (v[:, 0:D] + v[:, D : 2 * D]) + (w[:, 0:D] + w[:, D : 2 * D])
            acc[at, :] += jnp.dot(
                jnp.concatenate([v.astype(BF), w.astype(BF)], axis=1), jnp.concatenate(gs, axis=0), preferred_element_type=F32
            )
            return carry

        lax.fori_loop(0, 2, quad, 0, unroll=2)

    def partner_ready(t):
        for way in (0, 1):
            zz, h = block_of(t, way)
            from_partner(zz, h).wait_recv()

    def dist_of(s):
        return (0, 7, 1, 6, 2, 5, 3, 4)[s]

    def part(s):
        at = pl.ds(s * PT, PT)
        total = jnp.sum(sw[at, :], axis=1, keepdims=True)
        return acc[at, :] - total * rg[at, :].astype(F32)

    def t_copy(s):
        k = dist_of(s)
        there = (0, 2, 1, 4, 3, 6, 5, 7)[s]
        return remote(t_send.at[s], t_in.at[there], send_t.at[s], recv_t.at[there], at_y((y + k) % NY))

    def main(j, carry):
        t = jnp.where(j < 3, j, jnp.where(j < 6, j - 3, 3 + (j - 6) // 2))
        half = jnp.where(j < 3, 0, jnp.where(j < 6, 1, jnp.where(j < 14, j % 2, 15 - j)))
        even = j % 2 == 0
        first = jnp.logical_or(j < 3, jnp.logical_and(j >= 6, even))

        @pl.when(j == 3)
        def _():
            for s in range(4, 8):
                ready_rows(s)

        @pl.when(j == 15)
        def _():
            for s in (7, 6, 5, 4):
                t_send[s] = part(s).astype(BF)
            for s in (7, 6, 5, 4):
                t_copy(s).start()

        @pl.when(first)
        def _():
            partner_ready(t)

        tile(t, half)
        later = jnp.logical_and(even, jnp.logical_and(j >= 4, j <= 10))

        @pl.when(jnp.logical_or(j < 3, later))
        def _():
            arrivals(jnp.where(j < 3, j + 1, j // 2 + 2))

        return carry

    lax.fori_loop(0, 16, main, 0)

    for s in (3, 2, 1):
        t_send[s] = part(s).astype(BF)
    for s in (3, 2, 1):
        t_copy(s).start()
    total = part(0)
    for s in range(1, 8):
        remote(t_send.at[s], t_in.at[s], send_t.at[s], recv_t.at[s], partner).wait_recv()
        total += t_in[s].astype(F32)

    fg = total * scales[...]
    fg_buf[...] = fg
    fg_copy = pltpu.make_async_copy(fg_buf, fg_out, store.at[0])
    fg_copy.start()
    fgb = fg.astype(BF)
    part_out = jnp.dot(hid_t[...], fgb, preferred_element_type=F32).astype(BF)
    pg = lax.dot_general(fgb, w_out[...], NT, preferred_element_type=F32) * slope[...]
    pb = jnp.sum(pg, axis=0, keepdims=True)
    part_in = jnp.dot(pts_t[...], pg.astype(BF), preferred_element_type=F32).astype(BF)
    tilei = lax.broadcasted_iota(jnp.int32, (16, D), 0)

    def bias_tile(v):
        v_hi, v_mid, v_lo = split3(v)
        z16 = jnp.zeros((16, D), F32)
        return jnp.where(
            tilei == 0, v_hi.astype(F32), jnp.where(tilei == 1, v_mid.astype(F32), jnp.where(tilei == 2, v_lo.astype(F32), z16))
        ).astype(BF)

    for k in range(8):
        g[0, k, 0:PT, :] = part_out[k * PT : (k + 1) * PT, :]
        g[0, k, PT:PR, :] = jnp.zeros((16, D), BF)
        g[1, k, 0:PT, :] = part_in[:, k * D : (k + 1) * D]
        g[1, k, PT:PR, :] = bias_tile(jnp.broadcast_to(pb[:, k * D : (k + 1) * D], (16, D)))

    def at_1(k):
        return dev(jnp.where(c == 0, y, k), jnp.where(c == 0, k, z), x, c)

    def at_2(k):
        return dev(jnp.where(c == 0, k, y), jnp.where(c == 0, z, k), x, c)

    me1 = jnp.where(c == 0, z, y)
    me2 = jnp.where(c == 0, y, z)

    cuts = (pl.ds(0, 64), pl.ds(64, PR - 64))

    def put(ref, q, v):
        if q == 0:
            ref[0:64] = v.astype(BF)
        else:
            ref[64:PT] = v[0:64].astype(BF)
            ref[PT:PR] = bias_tile(jnp.broadcast_to(jnp.sum(v[64:72], axis=0, keepdims=True), (16, D)))

    def total_of(slots, n, q):
        tot = slots[0, cuts[q]].astype(F32)
        for k in range(1, n):
            tot += slots[k, cuts[q]].astype(F32)
        return tot

    def halves(q):
        return remote(g.at[1 - c, :, cuts[q]], x_in.at[:, cuts[q]], send_c.at[q], recv_c.at[q], partner)

    def outs(q):
        return remote(fin.at[c, :, cuts[q]], fin.at[c, :, cuts[q]], send_c.at[2 + q], recv_c.at[2 + q], partner)

    def outs_in(q):
        return remote(fin.at[1 - c, :, cuts[q]], fin.at[1 - c, :, cuts[q]], send_c.at[2 + q], recv_c.at[2 + q], partner)

    def line(peers, me, n, src_of, slots, ss, rs):
        def copy(q, k):
            to = (me + k) % n
            return remote(src_of(to).at[cuts[q]], slots.at[me, cuts[q]], ss.at[q, k], rs.at[q, me], peers(to))

        def source(q, k):
            at = (me + k) % n
            return remote(src_of(at).at[cuts[q]], slots.at[at, cuts[q]], ss.at[q, k], rs.at[q, at], peers(at))

        def go(q):
            for k in range(1, n):
                copy(q, k).start()

        def come(q):
            for k in range(1, n):
                source(q, k).wait_recv()

        def sent():
            for q in (0, 1):
                for k in range(1, n):
                    copy(q, k).wait_send()

        return go, come, sent

    go1, come1, sent1 = line(at_1, me1, 8, lambda k: s1.at[k], in1, send_1, recv_1)
    go2, come2, sent2 = line(at_2, me2, 8, lambda k: in2.at[me2], in2, send_2, recv_2)
    go3, come3, sent3 = line(at_x, x, NX, lambda k: in3.at[x], in3, send_3, recv_3)
    go4, come4, sent4 = line(at_1, me1, 8, lambda k: fin.at[c, me1], fin.at[c], send_4, recv_4)
    for q in (0, 1):
        halves(q).start()
    for k in (1, 3, 2):
        x_copy(z, k).wait_send()
    for k in range(1, 8):
        y_copy(k).wait_send()
        t_copy(k).wait_send()

    def sent(i, carry):
        zz, h = i // 2, i % 2
        back = (z + NZ - zz) % NZ
        ahead = (zz + NZ - z) % NZ

        @pl.when(c == 0)
        def _():
            @pl.when(jnp.logical_or(back < 3, jnp.logical_and(back == 3, h == 0)))
            def _():
                z_right(zz, h).wait_send()

            @pl.when(jnp.logical_or(ahead < 3, jnp.logical_and(ahead == 3, h == 1)))
            def _():
                z_left(zz, h).wait_send()

        to_partner(zz, h).wait_send()
        return carry

    lax.fori_loop(0, NZ * 2, sent, 0)

    @pl.when(c == 1)
    def _():
        for k in range(1, NZ):
            z_direct(k).wait_send()
            for m in (1, 3, 2):
                x_copy((z + k) % NZ, m).wait_send()

    for q in (0, 1):
        halves(q).wait_recv()
        for k in range(8):
            put(s1.at[k], q, g[c, k, cuts[q]].astype(F32) + x_in[k, cuts[q]].astype(F32))
        in1[me1, cuts[q]] = s1[me1, cuts[q]]
        go1(q)
    for q in (0, 1):
        come1(q)
        put(in2.at[me2], q, total_of(in1, 8, q))
        go2(q)
    sent1()
    for q in (0, 1):
        halves(q).wait_send()
    for q in (0, 1):
        come2(q)
        put(in3.at[x], q, total_of(in2, 8, q))
        go3(q)
    sent2()
    for q in (0, 1):
        come3(q)
        put(fin.at[c, me1], q, total_of(in3, NX, q))
        go4(q)
    sent3()
    for q in (0, 1):
        come4(q)
        outs(q).start()
    for q in (0, 1):
        outs_in(q).wait_recv()

    fin_copy = pltpu.make_async_copy(fin, fin_out, store.at[1])
    fin_copy.start()
    fg_copy.wait()
    fin_copy.wait()

    sent4()
    for q in (0, 1):
        outs(q).wait_send()


def finish(fg_in, fin, fg_out, gi_out, gb_out, go_out):
    factor = 1.0 / 256.0
    fg_out[...] = fg_in[...]
    for k in range(8):
        go_out[k * PT : (k + 1) * PT, :] = factor * fin[0, k, 0:PT].astype(F32)
        gi_out[:, k * D : (k + 1) * D] = factor * fin[1, k, 0:PT].astype(F32)
        bt = fin[1, k, PT:PR].astype(F32)
        gb_out[k : k + 1, :] = factor * (bt[0:1] + bt[1:2] + bt[2:3])


def local(points, w_in, b_in, w_out, scales, left, right):
    vmem = pl.BlockSpec(memory_space=pltpu.VMEM)
    hbm = pl.BlockSpec(memory_space=pl.ANY)
    dma = pltpu.SemaphoreType.DMA
    piece = (PR, D)
    fg, sums = pl.pallas_call(
        body,
        out_shape=[
            jax.ShapeDtypeStruct((PT, D), F32),
            jax.ShapeDtypeStruct((2, 8) + piece, BF),
        ],
        in_specs=[hbm, hbm, vmem, hbm, vmem, hbm, hbm],
        out_specs=[hbm] * 2,
        scratch_shapes=[
            pltpu.VMEM((PT, D), BF),
            pltpu.VMEM((D, HID), BF),
            pltpu.VMEM((HID, D), BF),
            pltpu.VMEM((64, PT), BF),
            pltpu.VMEM((64, PT), BF),
            pltpu.VMEM((PT, D), F32),
            pltpu.VMEM((PT, HID), F32),
            pltpu.VMEM((HID, PT), BF),
            pltpu.VMEM((D, PT), BF),
            pltpu.VMEM((NY, PR, 2 * D), BF),
            pltpu.VMEM((NC, NZ, NX, PR, 2 * D), BF),
            pltpu.VMEM((NY * PT, D), BF),
            pltpu.VMEM((NY * PT, D), BF),
            pltpu.VMEM((NY * PT, D), F32),
            pltpu.VMEM((NY * PT, D), F32),
            pltpu.VMEM((NY * PT, D), F32),
            pltpu.VMEM((NY, PT, D), BF),
            pltpu.VMEM((NY, PT, D), BF),
            pltpu.VMEM((2, 8) + piece, BF),
            pltpu.VMEM((8,) + piece, BF),
            pltpu.VMEM((8,) + piece, BF),
            pltpu.VMEM((8,) + piece, BF),
            pltpu.VMEM((8,) + piece, BF),
            pltpu.VMEM((NX,) + piece, BF),
            pltpu.VMEM((2, 8) + piece, BF),
            dma((5,)), dma((2,)), dma((8,)), dma((8,)), dma((NZ, NX)),
            dma((8,)), dma((2, NZ, 2)), dma((NZ, NX)), dma((NZ, 2)), dma((NZ, 2)), dma((NZ, 2)),
            dma((8,)), dma((8,)), dma((4,)), dma((4,)),
            dma((2, 8)), dma((2, 8)), dma((2, 8)), dma((2, 8)), dma((2, 4)), dma((2, 4)), dma((2, 8)), dma((2, 8)),
        ],
        compiler_params=pltpu.CompilerParams(collective_id=0, has_side_effects=True),
        name="gp_grad",
    )(points, w_in, b_in.reshape(1, HID), w_out, scales.reshape(1, D), left.T, right.T)
    fg, gi, gb, go = pl.pallas_call(
        finish,
        out_shape=[
            jax.ShapeDtypeStruct((PT, D), F32),
            jax.ShapeDtypeStruct((D, HID), F32),
            jax.ShapeDtypeStruct((8, D), F32),
            jax.ShapeDtypeStruct((HID, D), F32),
        ],
        in_specs=[vmem] * 2,
        out_specs=[vmem] * 4,
        name="finish",
    )(fg, sums)
    return fg, gi, gb.reshape(HID), go


def solution(mesh):
    placed = (
        P(("blk", "row"), None),
        P(),
        P(),
        P(),
        P(),
        P(("blk", "row"), None),
        P(("blk", "row"), None),
    )
    return jax.shard_map(
        local,
        mesh=mesh,
        in_specs=placed,
        out_specs=(P(("blk", "row"), None), P(), P(), P()),
        check_vma=False,
    )
```

```python
import jax
import jax.numpy as jnp
from jax import lax
from jax.experimental import pallas as pl
from jax.experimental.pallas import tpu as pltpu
from jax.sharding import PartitionSpec as P

NX, NY, NZ, NC = 4, 8, 8, 2
PT = 128
PR = 144
D = 128
HID = 1024
HALF = 512
BF = jnp.bfloat16
F32 = jnp.float32
MESH = pl.DeviceIdType.MESH
NT = (((1,), (1,)), ((), ()))


def split3(v):
    hi = v.astype(BF)
    rest = v - hi.astype(F32)
    mid = rest.astype(BF)
    lo = (rest - mid.astype(F32)).astype(BF)
    return hi, mid, lo


def body(
    points_hbm, w_in_hbm, b_in, w_out_hbm, scales, left_hbm, right_hbm,
    fg_out, fin_out,
    points, w_in, w_out, left, right, fg_buf,
    slope, hid_t, pts_t, rows, cols, rg, rb, ni, acc, sw, t_send, t_in,
    g, x_in, s1, in1, in2, in3, fin,
    load, store, send_y, recv_y, send_x, send_d, send_z, recv_a, recv_r, send_p, recv_p,
    send_t, recv_t, send_c, recv_c, send_1, recv_1, send_2, recv_2, send_3, recv_3, send_4, recv_4,
):
    blk = lax.axis_index("blk")
    row = lax.axis_index("row")
    y_lo = blk // (NX * NZ)
    z = (blk // NX) % NZ
    x = blk % NX
    c = row % 2
    y = (row // 2) * 2 + y_lo

    def dev(y_, z_, x_, c_):
        return (((y_ % 2) * NZ + z_) * NX + x_, (y_ // 2) * 2 + c_)

    def at_y(k):
        return dev(k, z, x, c)

    def at_z(k):
        return dev(y, k, x, c)

    def at_x(k):
        return dev(y, z, k, c)

    partner = dev(y, z, x, 1 - c)
    nxt = at_z((z + 1) % NZ)
    prv = at_z((z + NZ - 1) % NZ)

    def remote(src, dst, ss, rs, device):
        return pltpu.make_async_remote_copy(
            src_ref=src, dst_ref=dst, send_sem=ss, recv_sem=rs, device_id=device, device_id_type=MESH
        )

    loads = [
        pltpu.make_async_copy(src, dst, load.at[k])
        for k, (src, dst) in enumerate(
            ((points_hbm, points), (w_in_hbm, w_in), (w_out_hbm, w_out), (left_hbm, left), (right_hbm, right))
        )
    ]
    for copy in loads:
        copy.start()

    bar = pltpu.get_barrier_semaphore()

    def hello(device):
        pl.semaphore_signal(bar, inc=1, device_id=device, device_id_type=MESH)

    hello(partner)
    for k in range(1, NX):
        hello(at_x((x + k) % NX))
    for k in range(1, NZ):
        hello(at_z((z + k) % NZ))
    for k in range(1, NY):
        hello(at_y((y + k) % NY))

    loads[0].wait()
    loads[1].wait()
    pts = points[...]
    pre = jnp.dot(pts, w_in[...], preferred_element_type=F32) + b_in[...]
    sig = jax.nn.sigmoid(pre)
    hidden = (pre * sig).astype(BF)
    loads[2].wait()
    feats = jnp.dot(hidden, w_out[...], preferred_element_type=F32)
    scaled = (feats * scales[...]).astype(BF)
    sf = scaled.astype(F32)
    sq = sf * sf
    sq_hi = sq.astype(BF)
    sq_lo = (sq - sq_hi.astype(F32)).astype(BF)
    ones = jnp.full((16, D), 0.5, BF)
    norm = lax.dot_general(ones, sq_hi, NT, preferred_element_type=F32) + lax.dot_general(
        ones, sq_lo, NT, preferred_element_type=F32
    )
    hi, mid, lo = split3(norm)
    which = lax.broadcasted_iota(jnp.int32, (16, D), 0)
    zero = jnp.zeros((16, D), F32)
    tail = jnp.where(
        which == 0, hi.astype(F32), jnp.where(which == 1, mid.astype(F32), jnp.where(which == 2, lo.astype(F32), zero))
    ).astype(BF)
    mine = cols.at[c, z, x]
    mine[0:PT, 0:D] = scaled
    loads[3].wait()
    loads[4].wait()
    mine[0:PT, D : 2 * D] = jnp.concatenate([left[...].astype(F32), right[...].astype(F32)], axis=0).T.astype(BF)
    mine[PT:PR, 0:D] = tail
    mine[PT:PR, D : 2 * D] = jnp.zeros((16, D), BF)

    pl.semaphore_wait(bar, 1 + (NX - 1) + (NZ - 1) + (NY - 1))

    def slot_y(k):
        return jnp.where(k == 4, 7, jnp.where(k == 0, 0, jnp.where(k > 4, 2 * (8 - k) - 1, 2 * k)))

    def piece(zz, xx):
        return cols.at[c, zz, xx]

    def duo(zz, h):
        return cols.at[c, zz, pl.ds(2 * h, 2)]

    def arrival(zz, xx):
        return remote(piece(zz, xx), piece(zz, xx), send_x.at[0, 0], recv_a.at[zz, xx], partner)

    def z_right(zz, h):
        return remote(duo(zz, h), duo(zz, h), send_z.at[0, zz, h], recv_r.at[zz, h], nxt)

    def z_left(zz, h):
        return remote(duo(zz, h), duo(zz, h), send_z.at[1, zz, h], recv_r.at[zz, h], prv)

    def z_one(way, zz):
        return remote(piece(zz, x), piece(zz, x), send_d.at[way, zz], recv_a.at[zz, x], prv if way else nxt)

    def x_copy(zz, k):
        return remote(piece(zz, x), piece(zz, x), send_x.at[zz, k], recv_a.at[zz, x], at_x((x + k) % NX))

    def to_partner(zz, h):
        return remote(duo(zz, h), duo(zz, h), send_p.at[zz, h], recv_p.at[zz, h], partner)

    def from_partner(zz, h):
        there = cols.at[1 - c, zz, pl.ds(2 * h, 2)]
        return remote(there, there, send_p.at[zz, h], recv_p.at[zz, h], partner)

    def y_copy(k):
        return remote(mine, rows.at[slot_y((8 - k) % 8)], send_y.at[k], recv_y.at[slot_y((8 - k) % 8)], at_y((y + k) % NY))

    def y_from(s):
        return remote(mine, rows.at[s], send_y.at[0], recv_y.at[s], partner)

    def ready_rows(s):
        if s > 0:
            y_from(s).wait_recv()
        gg = rows[s, 0:PT, 0:D]
        ab = rows[s, 0:PT, D : 2 * D].astype(F32)
        at = pl.ds(s * PT, PT)
        rg[at, :] = gg
        rb[at, :] = pltpu.roll(ab, 64, 1).astype(BF)
        gf = gg.astype(F32)
        ni[at, :] = jnp.broadcast_to(0.5 * jnp.sum(gf * gf, axis=1, keepdims=True), (PT, D))

    @pl.when(c == 0)
    def _():
        for k in (1, 3, 2):
            x_copy(z, k).start()

    for k in (1, 7, 2, 6, 3, 5, 4):
        y_copy(k).start()

    @pl.when(c == 1)
    def _():
        z_one(0, z).start()
        z_one(1, z).start()

    rows[0] = mine[...]
    ready_rows(0)
    slope[...] = sig * (1.0 + pre * (1.0 - sig))
    hid_t[...] = hidden.astype(F32).T.astype(BF)
    pts_t[...] = pts.astype(F32).T.astype(BF)
    acc[...] = jnp.zeros_like(acc)
    sw[...] = jnp.zeros_like(sw)

    @pl.when(c == 1)
    def _():
        for k in (1, 3, 2):
            x_copy(z, k).start()

    own = x // 2

    def ready_duo(h):
        @pl.when(c == 0)
        def _():
            z_right(z, h).start()
            z_left(z, h).start()

        to_partner(z, h).start()

    arrival(z, x + 1 - 2 * (x % 2)).wait_recv()
    ready_duo(own)
    for i in (0, 1):
        arrival(z, 2 * (1 - own) + i).wait_recv()
    ready_duo(1 - own)


    def spread(way, dist):
        zz = (z + dist) % NZ if way else (z + NZ - dist) % NZ
        arrival(zz, x).wait_recv()

        @pl.when(jnp.logical_or(dist < 3, jnp.logical_and(dist == 3, x % 2 == way)))
        def _():
            z_one(way, zz).start()

        for k in (1, 3, 2):
            x_copy(zz, k).start()

    @pl.when(c == 1)
    def _():
        spread(0, 1)
        spread(1, 1)

    for s in range(1, 4):
        ready_rows(s)

    @pl.when(c == 1)
    def _():
        spread(0, 2)
        spread(1, 2)


    def block_of(t, way):
        edge = jnp.logical_or(t == 0, t == 7)
        dist = (t + 1) // 2
        zz = jnp.where(way == 0, (z + NZ - dist) % NZ, (z + dist) % NZ)
        h = jnp.where(edge, way, (t + 1) % 2)
        return zz, h

    def arrivals(t):
        dist = (t + 1) // 2

        @pl.when(c == 0)
        def _():
            for way in (0, 1):
                zz, h = block_of(t, way)
                on = jnp.logical_or(dist + 1 < 4, jnp.logical_and(dist == 3, h == way))
                hop = z_right(zz, h) if way == 0 else z_left(zz, h)
                hop.wait_recv()

                @pl.when(on)
                def _():
                    hop.start()

                to_partner(zz, h).start()

        @pl.when(c == 1)
        def _():
            @pl.when(t == 2)
            def _():
                spread(0, 3)
                spread(1, 3)

            @pl.when(t == 4)
            def _():
                spread(0, 4)

            for way in (0, 1):
                zz, h = block_of(t, way)
                for i in (0, 1):
                    xx = 2 * h + i

                    @pl.when(xx != x)
                    def _():
                        arrival(zz, xx).wait_recv()

                to_partner(zz, h).start()

    def tile(t, half):
        at = pl.ds(pl.multiple_of(half * HALF, HALF), HALF)
        nh = ni[at, :]
        nh2 = jnp.concatenate([nh, nh], axis=1)

        def quad(q, carry):
            cc = (c + q) % 2
            weights, gs = [], []
            for way in (0, 1):
                zz, h = block_of(t, way)
                both = pl.ds(2 * h, 2)
                cg = cols[cc, zz, both, 0:PT, 0:D].reshape(2 * PT, D)
                cb = cols[cc, zz, both, 0:PT, D : 2 * D].reshape(2 * PT, D)
                nt = cols[cc, zz, both, PT:PR, 0:D].astype(F32)
                nj = jnp.concatenate([nt[0, 0:1] + nt[0, 1:2] + nt[0, 2:3], nt[1, 0:1] + nt[1, 1:2] + nt[1, 2:3]], axis=1)
                cross = lax.dot_general(rg[at, :], cg, NT, preferred_element_type=F32)
                coup = lax.dot_general(rb[at, :], cb, NT, preferred_element_type=F32)
                weights.append(coup * jnp.exp(cross - nh2 - nj))
                gs.append(cg)
            v, w = weights
            sw[at, :] += (v[:, 0:D] + v[:, D : 2 * D]) + (w[:, 0:D] + w[:, D : 2 * D])
            acc[at, :] += jnp.dot(
                jnp.concatenate([v.astype(BF), w.astype(BF)], axis=1), jnp.concatenate(gs, axis=0), preferred_element_type=F32
            )
            return carry

        lax.fori_loop(0, 2, quad, 0, unroll=2)

    def partner_ready(t):
        for way in (0, 1):
            zz, h = block_of(t, way)
            from_partner(zz, h).wait_recv()

    def dist_of(s):
        return (0, 7, 1, 6, 2, 5, 3, 4)[s]

    def part(s):
        at = pl.ds(s * PT, PT)
        total = jnp.sum(sw[at, :], axis=1, keepdims=True)
        return acc[at, :] - total * rg[at, :].astype(F32)

    def t_copy(s):
        k = dist_of(s)
        there = (0, 2, 1, 4, 3, 6, 5, 7)[s]
        return remote(t_send.at[s], t_in.at[there], send_t.at[s], recv_t.at[there], at_y((y + k) % NY))

    def main(j, carry):
        t = jnp.where(j < 3, j, jnp.where(j < 6, j - 3, jnp.where(j < 12, 3 + (j - 6) // 2, 6 + j % 2)))
        half = jnp.where(j < 3, 0, jnp.where(j < 6, 1, jnp.where(j < 12, j % 2, 1 - (j - 12) // 2)))
        even = j % 2 == 0
        first = jnp.logical_or(j < 3, jnp.logical_or(jnp.logical_and(jnp.logical_and(j >= 6, j < 12), even), jnp.logical_or(j == 12, j == 13)))

        @pl.when(j == 3)
        def _():
            for s in range(4, 8):
                ready_rows(s)

        @pl.when(j == 14)
        def _():
            for s in (7, 6, 5, 4):
                t_send[s] = part(s).astype(BF)
            for s in (7, 6, 5, 4):
                t_copy(s).start()

        @pl.when(first)
        def _():
            partner_ready(t)

        tile(t, half)
        later = jnp.logical_and(even, jnp.logical_and(j >= 4, j <= 10))

        @pl.when(jnp.logical_or(j < 3, later))
        def _():
            arrivals(jnp.where(j < 3, j + 1, j // 2 + 2))

        return carry

    lax.fori_loop(0, 16, main, 0)

    for s in (3, 2, 1):
        t_send[s] = part(s).astype(BF)
    for s in (3, 2, 1):
        t_copy(s).start()
    total = part(0)
    for s in range(1, 8):
        remote(t_send.at[s], t_in.at[s], send_t.at[s], recv_t.at[s], partner).wait_recv()
        total += t_in[s].astype(F32)

    fg = total * scales[...]
    fg_buf[...] = fg
    fg_copy = pltpu.make_async_copy(fg_buf, fg_out, store.at[0])
    fg_copy.start()
    fgb = fg.astype(BF)
    part_out = jnp.dot(hid_t[...], fgb, preferred_element_type=F32).astype(BF)
    pg = lax.dot_general(fgb, w_out[...], NT, preferred_element_type=F32) * slope[...]
    pb = jnp.sum(pg, axis=0, keepdims=True)
    part_in = jnp.dot(pts_t[...], pg.astype(BF), preferred_element_type=F32).astype(BF)
    tilei = lax.broadcasted_iota(jnp.int32, (16, D), 0)

    def bias_tile(v):
        v_hi, v_mid, v_lo = split3(v)
        z16 = jnp.zeros((16, D), F32)
        return jnp.where(
            tilei == 0, v_hi.astype(F32), jnp.where(tilei == 1, v_mid.astype(F32), jnp.where(tilei == 2, v_lo.astype(F32), z16))
        ).astype(BF)

    for k in range(8):
        g[0, k, 0:PT, :] = part_out[k * PT : (k + 1) * PT, :]
        g[0, k, PT:PR, :] = jnp.zeros((16, D), BF)
        g[1, k, 0:PT, :] = part_in[:, k * D : (k + 1) * D]
        g[1, k, PT:PR, :] = bias_tile(jnp.broadcast_to(pb[:, k * D : (k + 1) * D], (16, D)))

    def at_1(k):
        return dev(jnp.where(c == 0, y, k), jnp.where(c == 0, k, z), x, c)

    def at_2(k):
        return dev(jnp.where(c == 0, k, y), jnp.where(c == 0, z, k), x, c)

    me1 = jnp.where(c == 0, z, y)
    me2 = jnp.where(c == 0, y, z)

    cuts = (pl.ds(0, 64), pl.ds(64, PR - 64))

    def put(ref, q, v):
        if q == 0:
            ref[0:64] = v.astype(BF)
        else:
            ref[64:PT] = v[0:64].astype(BF)
            ref[PT:PR] = bias_tile(jnp.broadcast_to(jnp.sum(v[64:72], axis=0, keepdims=True), (16, D)))

    def total_of(slots, n, q):
        tot = slots[0, cuts[q]].astype(F32)
        for k in range(1, n):
            tot += slots[k, cuts[q]].astype(F32)
        return tot

    def halves(q):
        return remote(g.at[1 - c, :, cuts[q]], x_in.at[:, cuts[q]], send_c.at[q], recv_c.at[q], partner)

    def outs(q):
        return remote(fin.at[c, :, cuts[q]], fin.at[c, :, cuts[q]], send_c.at[2 + q], recv_c.at[2 + q], partner)

    def outs_in(q):
        return remote(fin.at[1 - c, :, cuts[q]], fin.at[1 - c, :, cuts[q]], send_c.at[2 + q], recv_c.at[2 + q], partner)

    def line(peers, me, n, src_of, slots, ss, rs):
        def copy(q, k):
            to = (me + k) % n
            return remote(src_of(to).at[cuts[q]], slots.at[me, cuts[q]], ss.at[q, k], rs.at[q, me], peers(to))

        def source(q, k):
            at = (me + k) % n
            return remote(src_of(at).at[cuts[q]], slots.at[at, cuts[q]], ss.at[q, k], rs.at[q, at], peers(at))

        def go(q):
            for k in range(1, n):
                copy(q, k).start()

        def come(q):
            for k in range(1, n):
                source(q, k).wait_recv()

        def sent():
            for q in (0, 1):
                for k in range(1, n):
                    copy(q, k).wait_send()

        return go, come, sent

    go1, come1, sent1 = line(at_1, me1, 8, lambda k: s1.at[k], in1, send_1, recv_1)
    go2, come2, sent2 = line(at_2, me2, 8, lambda k: in2.at[me2], in2, send_2, recv_2)
    go3, come3, sent3 = line(at_x, x, NX, lambda k: in3.at[x], in3, send_3, recv_3)
    go4, come4, sent4 = line(at_1, me1, 8, lambda k: fin.at[c, me1], fin.at[c], send_4, recv_4)
    for q in (0, 1):
        halves(q).start()
    for k in (1, 3, 2):
        x_copy(z, k).wait_send()
    for k in range(1, 8):
        y_copy(k).wait_send()
        t_copy(k).wait_send()

    def sent(i, carry):
        zz, h = i // 2, i % 2
        back = (z + NZ - zz) % NZ
        ahead = (zz + NZ - z) % NZ

        @pl.when(c == 0)
        def _():
            @pl.when(jnp.logical_or(back < 3, jnp.logical_and(back == 3, h == 0)))
            def _():
                z_right(zz, h).wait_send()

            @pl.when(jnp.logical_or(ahead < 3, jnp.logical_and(ahead == 3, h == 1)))
            def _():
                z_left(zz, h).wait_send()

        to_partner(zz, h).wait_send()
        return carry

    lax.fori_loop(0, NZ * 2, sent, 0)

    @pl.when(c == 1)
    def _():
        for way in (0, 1):
            for d in range(3):
                z_one(way, (z + d) % NZ if way else (z + NZ - d) % NZ).wait_send()

            @pl.when(x % 2 == way)
            def _():
                z_one(way, (z + 3) % NZ if way else (z + NZ - 3) % NZ).wait_send()

        for k in range(1, NZ):
            for m in (1, 3, 2):
                x_copy((z + k) % NZ, m).wait_send()

    for q in (0, 1):
        halves(q).wait_recv()
        for k in range(8):
            put(s1.at[k], q, g[c, k, cuts[q]].astype(F32) + x_in[k, cuts[q]].astype(F32))
        in1[me1, cuts[q]] = s1[me1, cuts[q]]
        go1(q)
    for q in (0, 1):
        come1(q)
        put(in2.at[me2], q, total_of(in1, 8, q))
        go2(q)
    sent1()
    for q in (0, 1):
        halves(q).wait_send()
    for q in (0, 1):
        come2(q)
        put(in3.at[x], q, total_of(in2, 8, q))
        go3(q)
    sent2()
    for q in (0, 1):
        come3(q)
        put(fin.at[c, me1], q, total_of(in3, NX, q))
        go4(q)
    sent3()
    for q in (0, 1):
        come4(q)
        outs(q).start()
    for q in (0, 1):
        outs_in(q).wait_recv()

    fin_copy = pltpu.make_async_copy(fin, fin_out, store.at[1])
    fin_copy.start()
    fg_copy.wait()
    fin_copy.wait()

    sent4()
    for q in (0, 1):
        outs(q).wait_send()


def finish(fg_in, fin, fg_out, gi_out, gb_out, go_out):
    factor = 1.0 / 256.0
    fg_out[...] = fg_in[...]
    for k in range(8):
        go_out[k * PT : (k + 1) * PT, :] = factor * fin[0, k, 0:PT].astype(F32)
        gi_out[:, k * D : (k + 1) * D] = factor * fin[1, k, 0:PT].astype(F32)
        bt = fin[1, k, PT:PR].astype(F32)
        gb_out[k : k + 1, :] = factor * (bt[0:1] + bt[1:2] + bt[2:3])


def local(points, w_in, b_in, w_out, scales, left, right):
    vmem = pl.BlockSpec(memory_space=pltpu.VMEM)
    hbm = pl.BlockSpec(memory_space=pl.ANY)
    dma = pltpu.SemaphoreType.DMA
    piece = (PR, D)
    fg, sums = pl.pallas_call(
        body,
        out_shape=[
            jax.ShapeDtypeStruct((PT, D), F32),
            jax.ShapeDtypeStruct((2, 8) + piece, BF),
        ],
        in_specs=[hbm, hbm, vmem, hbm, vmem, hbm, hbm],
        out_specs=[hbm] * 2,
        scratch_shapes=[
            pltpu.VMEM((PT, D), BF),
            pltpu.VMEM((D, HID), BF),
            pltpu.VMEM((HID, D), BF),
            pltpu.VMEM((64, PT), BF),
            pltpu.VMEM((64, PT), BF),
            pltpu.VMEM((PT, D), F32),
            pltpu.VMEM((PT, HID), F32),
            pltpu.VMEM((HID, PT), BF),
            pltpu.VMEM((D, PT), BF),
            pltpu.VMEM((NY, PR, 2 * D), BF),
            pltpu.VMEM((NC, NZ, NX, PR, 2 * D), BF),
            pltpu.VMEM((NY * PT, D), BF),
            pltpu.VMEM((NY * PT, D), BF),
            pltpu.VMEM((NY * PT, D), F32),
            pltpu.VMEM((NY * PT, D), F32),
            pltpu.VMEM((NY * PT, D), F32),
            pltpu.VMEM((NY, PT, D), BF),
            pltpu.VMEM((NY, PT, D), BF),
            pltpu.VMEM((2, 8) + piece, BF),
            pltpu.VMEM((8,) + piece, BF),
            pltpu.VMEM((8,) + piece, BF),
            pltpu.VMEM((8,) + piece, BF),
            pltpu.VMEM((8,) + piece, BF),
            pltpu.VMEM((NX,) + piece, BF),
            pltpu.VMEM((2, 8) + piece, BF),
            dma((5,)), dma((2,)), dma((8,)), dma((8,)), dma((NZ, NX)),
            dma((2, NZ)), dma((2, NZ, 2)), dma((NZ, NX)), dma((NZ, 2)), dma((NZ, 2)), dma((NZ, 2)),
            dma((8,)), dma((8,)), dma((4,)), dma((4,)),
            dma((2, 8)), dma((2, 8)), dma((2, 8)), dma((2, 8)), dma((2, 4)), dma((2, 4)), dma((2, 8)), dma((2, 8)),
        ],
        compiler_params=pltpu.CompilerParams(collective_id=0, has_side_effects=True),
        name="gp_grad",
    )(points, w_in, b_in.reshape(1, HID), w_out, scales.reshape(1, D), left.T, right.T)
    fg, gi, gb, go = pl.pallas_call(
        finish,
        out_shape=[
            jax.ShapeDtypeStruct((PT, D), F32),
            jax.ShapeDtypeStruct((D, HID), F32),
            jax.ShapeDtypeStruct((8, D), F32),
            jax.ShapeDtypeStruct((HID, D), F32),
        ],
        in_specs=[vmem] * 2,
        out_specs=[vmem] * 4,
        name="finish",
    )(fg, sums)
    return fg, gi, gb.reshape(HID), go


def solution(mesh):
    placed = (
        P(("blk", "row"), None),
        P(),
        P(),
        P(),
        P(),
        P(("blk", "row"), None),
        P(("blk", "row"), None),
    )
    return jax.shard_map(
        local,
        mesh=mesh,
        in_specs=placed,
        out_specs=(P(("blk", "row"), None), P(), P(), P()),
        check_vma=False,
    )
```
